32 devices in a mesh: dp: 4 (over y, x), seq: 2 (over core), tensor: 4 (over z).
Axes of the slice: x: 2, y: 2, z: 4, core: 2. Of those that a mesh axis runs over, the one named last changes fastest.
Arguments:
- entry_x: bfloat16 [48, 512, 1024], P('dp', 'seq', 'tensor'), may hold values from -6 to 6
- entry_z: bfloat16 [48, 512, 1024], P('dp', 'seq', 'tensor'), may hold values from -6 to 6
- entry_bc: bfloat16 [48, 512, 256], P('dp', 'seq'), may hold values from -6 to 6
- entry_dt: bfloat16 [48, 512, 16], P('dp', 'seq', 'tensor'), may hold values from -3 to 3
- source_rank: int32 [4, 4], replicated, may hold values from 0 to 3, as said below
- source_slot: int32 [4, 4], replicated, may hold values from 0 to 11, as said below
- row_spans: int32 [4, 4], replicated, may hold values from 0 to 4, as said below
- conv_x_weight: float32 [4, 1024], P(None, 'tensor'), may hold values from -3 to 3
- conv_x_bias: float32 [1024], P('tensor'), may hold values from -2 to 2
- conv_bc_weight: float32 [4, 256], replicated, may hold values from -3 to 3
- conv_bc_bias: float32 [256], replicated, may hold values from -2 to 2
- dt_bias: float32 [16], P('tensor'), may hold values from -0.5 to 0.5
- a_log: float32 [16], P('tensor')
- d_skip: float32 [16], P('tensor'), may hold values from 0.5 to 1.5
- norm_gain: float32 [1024], P('tensor'), may hold values from 0.1 to 1.9
- out_weight: bfloat16 [1024, 4096], P('tensor'), may hold values from -0.1875 to 0.1875
Outputs:
- mixed: bfloat16 [16, 512, 4096], P('dp', 'seq', 'tensor')
The draws below stay inside these ranges and needn't reach their ends.
Inputs may be any that keep to these rules, and one draw needn't show every extreme that they name: `source_rank`: each slot's block is held on entry by its own data rank or by a data rank next to it; no entry slot serves two slots. `source_slot`: together with source_rank: an entry slot of the named data rank. `row_spans`: on every data rank the nonzero lengths come first and sum to 4.
All inputs are finite; a program needn't handle non-finite values.
Results may differ from the reference program's by a relative error of at most 0.0095.
Values may be sent and summed in bfloat16 or wider, within the bound.
A program may use at most 128 MiB of HBM per device.

```python
import jax
import jax.numpy as jnp
from jax import lax

OUT_COLS = 4096
HEAD = 64
STATE = 128
CONV = 4
BLOCK = 256
BIN = 4
HEADS = 16
INNER = 1024
ROWS_IN = 48
SEQ_LEN = 512
N_DP = 4
N_SEQ = 2
N_TENSOR = 4


def loader_tables(key):
    base_key = jax.random.fold_in(key, 7)
    offsets = jax.random.randint(jax.random.fold_in(base_key, 1), (N_DP, BIN), -1, 2)
    rank_ids = jnp.arange(N_DP)[:, None]
    slot_ids_grid = jnp.arange(BIN)[None, :]
    offsets = jnp.where((slot_ids_grid == 0) & (rank_ids > 0), -1, offsets)
    offsets = jnp.where((slot_ids_grid == 1) & (rank_ids < N_DP - 1), 1, offsets)
    offsets = jnp.where(rank_ids == 0, jnp.maximum(offsets, 0), offsets)
    offsets = jnp.where(rank_ids == N_DP - 1, jnp.minimum(offsets, 0), offsets)
    sources = rank_ids + offsets
    perm_keys = jax.random.split(jax.random.fold_in(base_key, 2), N_DP)
    orders = jax.vmap(lambda single: jax.random.permutation(single, 3 * BIN))(perm_keys)
    wanted = (1 - offsets) * BIN + slot_ids_grid
    slot_ids = orders[sources, wanted]
    return (sources.astype(jnp.int32), slot_ids.astype(jnp.int32))


def draw_source_rank(key, part):
    return loader_tables(key)[0]


def draw_source_slot(key, part):
    return loader_tables(key)[1]


def draw_row_spans(key, part):
    flags = jax.random.randint(jax.random.fold_in(key, 11), (N_DP, BIN), 0, 2)
    leading = (jnp.arange(BIN) == 0).astype(jnp.int32)[None, :]
    flags = jnp.maximum(flags, leading)
    flags = jnp.where(jnp.arange(N_DP)[:, None] == 0, leading, flags)
    row_ids = jnp.cumsum(flags, axis=1) - 1
    counted = row_ids[:, :, None] == jnp.arange(BIN)[None, None, :]
    return jnp.sum(counted.astype(jnp.int32), axis=1).astype(jnp.int32)


def draw_a_log(key, part):
    chain_len = BIN * N_SEQ * BLOCK
    spread = jax.random.uniform(jax.random.fold_in(key, 13), (HEADS,), jnp.float32)
    slowest = jnp.log(0.3 / chain_len)
    rates = slowest + spread * (jnp.log(1.0 / 35.0) - slowest)
    return (rates - jnp.log(0.7)).astype(jnp.float32)


def block_levels(stream_key, extent, cuts, low, largest):
    def one(axis_at, parts):
        heights = jax.random.uniform(jax.random.fold_in(jax.random.fold_in(stream_key, 6), axis_at), (parts,), jnp.float32, low / len(cuts), largest / len(cuts))
        return jnp.repeat(jnp.exp(heights), extent[axis_at] // parts).reshape((-1,) + (1,) * (len(extent) - axis_at - 1))

    loudness = one(*cuts[0])
    for cut in cuts[1:]:
        loudness = loudness * one(*cut)
    return loudness


def normal_values(rng, shape, scale, reach, cuts=(), kind=jnp.bfloat16):
    factor_of = block_levels(rng, shape, cuts, -0.22, 0.18) if cuts else 1.0
    array = jax.random.normal(rng, shape, jnp.float32) * scale * factor_of
    return jnp.minimum(jnp.maximum(array, -reach), reach).astype(kind)


def setup_inputs(seed: int = 0) -> dict:
    key_list = jax.random.split(jax.random.key(seed), 17)
    return {
        "entry_x": normal_values(key_list[0], (ROWS_IN, SEQ_LEN, INNER), 1.0, 6.0, ((0, 4), (1, 2), (2, 4))),
        "entry_z": normal_values(key_list[1], (ROWS_IN, SEQ_LEN, INNER), 1.0, 6.0, ((0, 4), (1, 2), (2, 4))),
        "entry_bc": normal_values(key_list[2], (ROWS_IN, SEQ_LEN, 2 * STATE), 1.0, 6.0, ((0, 4), (1, 2))),
        "entry_dt": normal_values(key_list[3], (ROWS_IN, SEQ_LEN, HEADS), 0.5, 3.0, ((0, 4), (1, 2), (2, 4))),
        "source_rank": draw_source_rank(jax.random.fold_in(key_list[16], 71), 0),
        "source_slot": draw_source_slot(jax.random.fold_in(key_list[16], 71), 0),
        "row_spans": draw_row_spans(jax.random.fold_in(key_list[16], 71), 0),
        "conv_x_weight": normal_values(key_list[7], (CONV, INNER), 0.5, 3.0, ((1, 4),), jnp.float32),
        "conv_x_bias": normal_values(key_list[8], (INNER,), 0.3, 2.0, ((0, 4),), jnp.float32),
        "conv_bc_weight": normal_values(key_list[9], (CONV, 2 * STATE), 0.5, 3.0, (), jnp.float32),
        "conv_bc_bias": normal_values(key_list[10], (2 * STATE,), 0.3, 2.0, (), jnp.float32),
        "dt_bias": jnp.clip(jax.random.uniform(key_list[11], (HEADS,), jnp.float32, -0.5, 0.5) * block_levels(key_list[11], (HEADS,), ((0, 4),), -0.4, 0.0), -0.5, 0.5),
        "a_log": draw_a_log(jax.random.fold_in(key_list[16], 71), 0),
        "d_skip": jnp.clip(0.5 + 1.0 * jax.random.uniform(key_list[13], (HEADS,), jnp.float32) ** block_levels(key_list[13], (HEADS,), ((0, 4),), -0.2, 0.2), 0.5, 1.5),
        "norm_gain": jnp.clip(1.0 + 0.18 * jax.random.normal(key_list[14], (INNER,), jnp.float32), 0.1, 1.9),
        "out_weight": normal_values(key_list[15], (INNER, OUT_COLS), INNER ** -0.5, 0.1875, ((0, 4),)),
    }


norm_epsilon = 1e-05
highest = lax.Precision.HIGHEST

def row_layout(lengths):
    bin_count = lengths.shape[0]
    position = jnp.arange(bin_count, dtype=jnp.int32)
    starts = (jnp.cumsum(lengths) - lengths).astype(jnp.int32)
    present = lengths > 0
    opens_row = jnp.any(present[:, None] & (starts[:, None] == position[None, :]), axis=0)
    ending = (starts + lengths - 1).astype(jnp.int32)
    closes_row = jnp.any(present[:, None] & (ending[:, None] == position[None, :]), axis=0)
    row_of = (jnp.cumsum(opens_row.astype(jnp.int32)) - 1).astype(jnp.int32)
    row_owner = row_of[:, None] == position[None, :]
    final_slot = lax.optimization_barrier(jnp.sum(jnp.where(row_owner, ending[None, :], 0), axis=1)).astype(jnp.int32)
    return (opens_row, closes_row, row_of, row_owner, final_slot)

def causal_conv(before_rows, raw_input, weight, bias_vec):
    tap_count = weight.shape[0]
    piece_len = raw_input.shape[1]
    joined = jnp.concatenate([before_rows, raw_input], 1).astype(jnp.float32)
    running = bias_vec.astype(jnp.float32)
    for tap_index in range(tap_count):
        running = running + weight[tap_index].astype(jnp.float32) * joined[:, tap_index:tap_index + piece_len]
    return jax.nn.silu(running).astype(jnp.bfloat16)

def block_local(xc, bc_act, dt_raw, a_log, dt_bias, head_width):
    piece_count, piece_len, inner_width = xc.shape
    head_count = inner_width // head_width
    state_width = bc_act.shape[2] // 2
    b_part = bc_act[..., :state_width]
    c_part = bc_act[..., state_width:]
    step_size = jax.nn.softplus(dt_raw.astype(jnp.float32) + dt_bias)
    cumulative = jnp.cumsum(step_size * -jnp.exp(a_log), axis=1)
    gram_matrix = jnp.einsum('ktn,ksn->kts', c_part.astype(jnp.float32), b_part.astype(jnp.float32), precision=highest)
    cum_heads = jnp.swapaxes(cumulative, 1, 2)
    step_heads = jnp.swapaxes(step_size, 1, 2)
    lower_mask = jnp.arange(piece_len)[:, None] >= jnp.arange(piece_len)[None, :]
    log_gap = jnp.where(lower_mask, cum_heads[:, :, :, None] - cum_heads[:, :, None, :], -jnp.inf)
    mix_weights = (gram_matrix[:, None] * jnp.exp(log_gap) * step_heads[:, :, None, :]).astype(jnp.bfloat16)
    x_heads = xc.reshape(piece_count, piece_len, head_count, head_width)
    intra_out = jnp.einsum('khts,kshp->kthp', mix_weights.astype(jnp.float32), x_heads.astype(jnp.float32), precision=highest)
    tail_weight = jnp.exp(cumulative[:, -1:, :] - cumulative) * step_size
    weighted = (tail_weight[..., None] * b_part[:, :, None, :].astype(jnp.float32)).astype(jnp.bfloat16)
    contribution = jnp.einsum('kshp,kshn->khpn', x_heads.astype(jnp.float32), weighted.astype(jnp.float32), precision=highest)
    decay_total = jnp.exp(cumulative[:, -1, :])
    return (intra_out, cumulative, contribution, decay_total)

def finish(intra_out, cumulative, c_part, entering, xc, gate_in, d_skip, norm_gain, head_width, group_count):
    piece_count, piece_len, inner_width = xc.shape
    head_count = inner_width // head_width
    read_out = jnp.einsum('ktn,khpn->kthp', c_part.astype(jnp.float32), entering, precision=highest)
    x_heads = xc.reshape(piece_count, piece_len, head_count, head_width).astype(jnp.float32)
    output_raw = intra_out + jnp.exp(cumulative)[..., None] * read_out + d_skip[:, None] * x_heads
    group_width = inner_width // group_count
    gated_out = output_raw.reshape(piece_count, piece_len, group_count, group_width) * jax.nn.silu(gate_in.astype(jnp.float32)).reshape(piece_count, piece_len, group_count, group_width)
    inv_scale = lax.rsqrt(lax.optimization_barrier(jnp.mean(gated_out * gated_out, axis=-1, keepdims=True)) + norm_epsilon)
    return ((gated_out * inv_scale).reshape(piece_count, piece_len, inner_width) * norm_gain).astype(jnp.bfloat16)

def reference(entry_x, entry_z, entry_bc, entry_dt, source_rank, source_slot, row_spans, conv_x_weight, conv_x_bias, conv_bc_weight, conv_bc_bias, dt_bias, a_log, d_skip, norm_gain, out_weight):
    in_slots = 3 * BIN
    pick_rows = (source_rank * in_slots + source_slot).reshape(-1).astype(jnp.int32)

    def arrange(entry):
        chosen = jnp.take(entry, pick_rows, axis=0)
        chosen = chosen.reshape(N_DP, BIN, N_SEQ, BLOCK, entry.shape[-1])
        return jnp.transpose(chosen, (0, 2, 1, 3, 4))
    tap_weight = jnp.concatenate([conv_x_weight, conv_bc_weight], 1)
    tap_bias = jnp.concatenate([conv_x_bias, conv_bc_bias], 0)

    def one_bin(pieces):
        bin_x, bin_z, bin_bc, bin_dt, lengths = pieces
        opens_row, closes_row, row_of, row_owner, final_slot = row_layout(lengths)
        raw_input = jnp.concatenate([bin_x, bin_bc], -1)
        tail_rows = jnp.zeros((BIN, CONV - 1, raw_input.shape[-1]), jnp.bfloat16)
        activated = []
        for seq_index in range(N_SEQ):
            for slot_index in range(BIN):
                row_index = row_of[slot_index]
                before_rows = lax.dynamic_index_in_dim(tail_rows, row_index, 0, keepdims=True)
                piece_rows = raw_input[seq_index, slot_index][None]
                activated.append(causal_conv(before_rows, piece_rows, tap_weight, tap_bias)[0])
                tail_rows = lax.dynamic_update_index_in_dim(tail_rows, piece_rows[0, BLOCK - (CONV - 1):], row_index, 0)
        activated = jnp.stack(activated)
        xc = activated[..., :INNER]
        bc_act = activated[..., INNER:]
        intra_out, cumulative, contribution, decay_total = block_local(xc, bc_act, bin_dt.reshape(-1, BLOCK, HEADS), a_log, dt_bias, HEAD)
        carry_state = jnp.zeros((BIN, HEADS, HEAD, STATE), jnp.float32)
        entering = []
        for index in range(N_SEQ * BIN):
            row_index = row_of[index % BIN]
            state_in = lax.dynamic_index_in_dim(carry_state, row_index, 0, keepdims=False)
            entering.append(state_in)
            carry_state = lax.dynamic_update_index_in_dim(carry_state, decay_total[index][:, None, None] * state_in + contribution[index], row_index, 0)
        normed = finish(intra_out, cumulative, bc_act[..., STATE:], jnp.stack(entering), xc, bin_z.reshape(-1, BLOCK, INNER), d_skip, norm_gain, HEAD, N_TENSOR)
        return normed.reshape(N_SEQ, BIN, BLOCK, INNER)
    normed_all = lax.map(one_bin, (arrange(entry_x), arrange(entry_z), arrange(entry_bc), arrange(entry_dt), row_spans))
    normed_rows = jnp.transpose(normed_all, (0, 2, 1, 3, 4)).reshape(N_DP * BIN, N_SEQ * BLOCK, INNER)
    inner_dev = INNER // N_TENSOR

    def project(block_rows):
        running = jnp.zeros((block_rows.shape[0], OUT_COLS), jnp.float32)
        for group_index in range(N_TENSOR):
            group_part = jnp.dot(block_rows[:, group_index * inner_dev:(group_index + 1) * inner_dev], out_weight[group_index * inner_dev:(group_index + 1) * inner_dev], preferred_element_type=jnp.float32)
            running = running + lax.optimization_barrier(group_part.astype(jnp.bfloat16)).astype(jnp.float32)
        return running.astype(jnp.bfloat16)
    return lax.map(project, normed_rows)
```

```python
import functools

import jax
import jax.numpy as jnp
from jax import lax
from jax.experimental import pallas as pl
from jax.experimental.pallas import tpu as pltpu
from jax.sharding import PartitionSpec as P

HEAD = 64
EXTRA = 16
EPS = 1e-05
F32 = jnp.float32
BF16 = jnp.bfloat16
HIGHEST = lax.Precision.HIGHEST


def shifted(value, axis, steps):
    count = lax.axis_size(axis)
    first, last = (max(0, -steps), min(count, count - steps))
    return lax.ppermute(value, axis, [(source, source + steps) for source in range(first, last)])


def pack_kernel(slot_ref, peer_ref, x_ref, z_ref, bc_ref, dt_ref, tail_ref, main_ref, gate_ref):
    length, width = x_ref.shape[1:]
    heads = dt_ref.shape[1]
    main_ref[0, :length, :width] = x_ref[0]
    main_ref[0, :length, width:] = bc_ref[0]
    main_ref[0, length:, :] = tail_ref[0]
    main_ref[0, length : length + heads, : dt_ref.shape[2]] = dt_ref[0]
    gate_ref[0] = z_ref[0]


def pack(source_slot, peer, entry_x, entry_z, entry_bc, dt_rows, tails):
    count = source_slot.shape[1]
    length, width = entry_x.shape[1:]
    full = width + entry_bc.shape[2]

    def spec(array):
        return pl.BlockSpec((1,) + array.shape[1:], lambda j, slots, who: (slots[who[0], j], 0, 0))

    def out(rows, cols):
        return pl.BlockSpec((1, rows, cols), lambda j, slots, who: (j, 0, 0))

    operands = (entry_x, entry_z, entry_bc, dt_rows, tails)
    return pl.pallas_call(
        pack_kernel,
        grid_spec=pltpu.PrefetchScalarGridSpec(
            num_scalar_prefetch=2,
            grid=(count,),
            in_specs=[spec(array) for array in operands],
            out_specs=[out(length + EXTRA, full), out(length, width)],
        ),
        out_shape=[
            jax.ShapeDtypeStruct((count, length + EXTRA, full), BF16),
            jax.ShapeDtypeStruct((count, length, width), BF16),
        ],
        cost_estimate=pl.CostEstimate(flops=0, bytes_accessed=4_000_000, transcendentals=0),
        name="pack",
    )(source_slot, peer, *operands)


def slot_row(spans_ref, rank, j, count):
    start, opens, final = jnp.int32(0), jnp.int32(0), jnp.int32(0)
    for k in range(count):
        span = spans_ref[rank, k]
        inside = (j >= start) & (j < start + span)
        opens = jnp.where(inside & (j == start), 1, opens)
        final = jnp.where(inside, start + span - 1, final)
        start = start + span
    return opens == 1, final


def choose(rank_of, rank, own, left, right):
    return jnp.where(rank_of == rank, own, jnp.where(rank_of < rank, left, right))


def scan_kernel(
    rank_ref, source_ref, spans_ref, dtb_ref, alog_ref, skip_ref,
    own_ref, left_ref, right_ref, wx_ref, wbc_ref, bx_ref, bbc_ref,
    base_ref, scale_ref, c_ref, end_ref,
    joined, tail, state, decay, mixes, spread, weighted,
):
    j = pl.program_id(0)
    rank = rank_ref[0]
    count = own_ref.shape[0]
    length = own_ref.shape[1] - EXTRA
    width = wx_ref.shape[1]
    bc_width = wbc_ref.shape[1]
    states = bc_width // 2
    taps = wx_ref.shape[0]
    heads = width // HEAD
    opens, final = slot_row(spans_ref, rank, j, count)

    def moved(slot, rows):
        parts = [ref[slot, rows, :].astype(F32) for ref in (own_ref, left_ref, right_ref)]
        return choose(source_ref[rank, slot], rank, *parts)

    before = moved(final, slice(length, length + EXTRA))[EXTRA - 8 :]
    joined[0:8, :] = jnp.where(opens, before, tail[...])
    joined[8 : 8 + length, :] = moved(j, slice(0, length))
    steps = moved(j, slice(length, length + EXTRA))[0:8, :length]
    tail[...] = joined[length : length + 8, :]

    def conv(weight_ref, bias_ref, first, last):
        total = bias_ref[...]
        for k in range(taps):
            offset = 8 - (taps - 1) + k
            total = total + weight_ref[k : k + 1, :] * joined[offset : offset + length, first:last]
        return (total / (1.0 + jnp.exp(-total))).astype(BF16)

    xc = conv(wx_ref, bx_ref, 0, width)
    bc = conv(wbc_ref, bbc_ref, width, width + bc_width)
    b_rows = jnp.transpose(bc[:, :states].astype(F32))
    c_act = bc[:, states:]
    c_ref[0] = c_act

    row = lax.broadcasted_iota(jnp.int32, (8, length), 0)
    shift = jnp.zeros((8, length), F32)
    rate = jnp.zeros((8, length), F32)
    for h in range(heads):
        shift = jnp.where(row == h, dtb_ref[h], shift)
        rate = jnp.where(row == h, alog_ref[h], rate)
    raw = steps + shift
    dt = jnp.maximum(raw, 0.0) + jnp.log1p(jnp.exp(-jnp.abs(raw)))
    rates = jnp.where(row < heads, -jnp.exp(rate) * dt, 0.0)
    t_at = lax.broadcasted_iota(jnp.int32, (length, length), 0)
    s_at = lax.broadcasted_iota(jnp.int32, (length, length), 1)
    lower = t_at >= s_at
    ones = jnp.where(lower, 1.0, 0.0).astype(BF16)
    hi = rates.astype(BF16)
    mid = (rates - hi.astype(F32)).astype(BF16)
    low = (rates - hi.astype(F32) - mid.astype(F32)).astype(BF16)
    across = (((1,), (1,)), ((), ()))
    cum_rows = sum(
        lax.dot_general(part, ones, across, preferred_element_type=F32) for part in (low, mid, hi)
    )
    padded = jnp.concatenate([cum_rows] + [jnp.zeros((120, length), F32)], 0)
    cum_cols = jnp.transpose(padded)
    total = cum_rows[:, length - 1 :]
    gone = jnp.exp(total - cum_rows) * dt

    gram = jnp.dot(c_act, b_rows.astype(BF16), preferred_element_type=F32)
    lane_head = lax.broadcasted_iota(jnp.int32, (length, width), 1) // HEAD
    cum_wide = jnp.zeros((length, width), F32)
    skip_wide = jnp.zeros((1, width), F32)
    for h in range(heads):
        column = cum_cols[:, h : h + 1]
        gap = jnp.where(lower, column - cum_rows[h : h + 1, :], -jnp.inf)
        mix = gram * jnp.exp(gap) * dt[h : h + 1, :]
        mixes[:, h * length : (h + 1) * length] = mix.astype(BF16)
        weighted[:, h * length : (h + 1) * length] = (gone[h : h + 1, :] * b_rows).astype(BF16)
        spread[h * length : (h + 1) * length, :] = jnp.where(
            lane_head == h, xc.astype(F32), 0.0
        ).astype(BF16)
        cum_wide = jnp.where(lane_head == h, column, cum_wide)
        skip_wide = jnp.where(lane_head[0:1] == h, skip_ref[h], skip_wide)
    intra = jnp.dot(mixes[...], spread[...], preferred_element_type=F32)
    contrib = jnp.dot(weighted[...], spread[...], preferred_element_type=F32)

    grown = jnp.exp(cum_wide)
    block_decay = grown[length - 1 : length, :]
    entering = jnp.where(opens, 0.0, state[...])
    passed = jnp.where(opens, 1.0, decay[...])
    ent_hi = entering.astype(BF16)
    ent_lo = (entering - ent_hi.astype(F32)).astype(BF16)
    read = jnp.dot(c_act, ent_hi, preferred_element_type=F32) + jnp.dot(
        c_act, ent_lo, preferred_element_type=F32
    )
    base_ref[0] = intra + grown * read + skip_wide * xc.astype(F32)
    scale_ref[0] = grown * passed
    ended = block_decay * entering + contrib
    state[...] = ended
    decay[...] = passed * block_decay
    end_ref[0] = ended


def scan(rank, source_rank, row_spans, dt_bias, a_log, d_skip, own, left, right, wx, wbc, bx, bbc):
    count, tall, full = own.shape
    length = tall - EXTRA
    width, bc_width = wx.shape[1], wbc.shape[1]
    heads, states = width // HEAD, bc_width // 2

    def whole(array):
        return pl.BlockSpec(array.shape, lambda j, *_: (0,) * array.ndim)

    def slot(rows, cols):
        return pl.BlockSpec((1, rows, cols), lambda j, *_: (j, 0, 0))

    return pl.pallas_call(
        scan_kernel,
        grid_spec=pltpu.PrefetchScalarGridSpec(
            num_scalar_prefetch=6,
            grid=(count,),
            in_specs=[whole(array) for array in (own, left, right, wx, wbc, bx, bbc)],
            out_specs=[
                slot(length, width), slot(length, width), slot(length, states), slot(states, width)
            ],
            scratch_shapes=[
                pltpu.VMEM((length + 8, full), F32),
                pltpu.VMEM((8, full), F32),
                pltpu.VMEM((states, width), F32),
                pltpu.VMEM((1, width), F32),
                pltpu.VMEM((length, heads * length), BF16),
                pltpu.VMEM((heads * length, width), BF16),
                pltpu.VMEM((states, heads * length), BF16),
            ],
        ),
        out_shape=[
            jax.ShapeDtypeStruct((count, length, width), F32),
            jax.ShapeDtypeStruct((count, length, width), F32),
            jax.ShapeDtypeStruct((count, length, states), BF16),
            jax.ShapeDtypeStruct((count, states, width), F32),
        ],
        compiler_params=pltpu.CompilerParams(vmem_limit_bytes=40 << 20),
        cost_estimate=pl.CostEstimate(
            flops=3_000_000_000, bytes_accessed=8_000_000, transcendentals=2_000_000
        ),
        name="scan",
    )(rank, source_rank, row_spans, dt_bias, a_log, d_skip, own, left, right, wx, wbc, bx, bbc)


def gate_kernel(
    rank_ref, source_ref, spans_ref,
    base_ref, scale_ref, c_ref, carried_ref, own_ref, left_ref, right_ref, gain_ref, out_ref,
):
    j = pl.program_id(0)
    rank = rank_ref[0]
    _, final = slot_row(spans_ref, rank, j, carried_ref.shape[0])
    carried = carried_ref[final]
    high = carried.astype(BF16)
    low = (carried - high.astype(F32)).astype(BF16)
    c_act = c_ref[0]
    read = jnp.dot(c_act, high, preferred_element_type=F32) + jnp.dot(
        c_act, low, preferred_element_type=F32
    )
    y = base_ref[0] + scale_ref[0] * read
    parts = [ref[0].astype(F32) for ref in (own_ref, left_ref, right_ref)]
    z = choose(source_ref[rank, j], rank, *parts)
    g = y * (z / (1.0 + jnp.exp(-z)))
    inverse = lax.rsqrt(jnp.mean(g * g, axis=-1, keepdims=True) + EPS)
    out_ref[0] = (g * inverse * gain_ref[...]).astype(BF16)


def gate(rank, source_rank, row_spans, base, scale, c_act, carried, own, left, right, gain):
    count, length, width = base.shape

    def whole(array):
        return pl.BlockSpec(array.shape, lambda j, *_: (0,) * array.ndim)

    def slot(array):
        return pl.BlockSpec((1,) + array.shape[1:], lambda j, *_: (j, 0, 0))

    return pl.pallas_call(
        gate_kernel,
        grid_spec=pltpu.PrefetchScalarGridSpec(
            num_scalar_prefetch=3,
            grid=(count,),
            in_specs=[slot(base), slot(scale), slot(c_act), whole(carried)]
            + [slot(own)] * 3
            + [whole(gain)],
            out_specs=slot(base),
        ),
        out_shape=jax.ShapeDtypeStruct((count, length, width), BF16),
        name="gate",
    )(rank, source_rank, row_spans, base, scale, c_act, carried, own, left, right, gain)


def project_kernel(rows_ref, weight_ref, out_ref):
    total = jnp.dot(rows_ref[0, 0], weight_ref[0], preferred_element_type=F32)
    for i in range(1, weight_ref.shape[0]):
        total = total + jnp.dot(rows_ref[i, 0], weight_ref[i], preferred_element_type=F32)
    out_ref[0] = total.astype(BF16)


def project(rows, weight):
    groups, count, length, width = rows.shape
    cols = weight.shape[2]
    return pl.pallas_call(
        project_kernel,
        grid=(count,),
        in_specs=[
            pl.BlockSpec((groups, 1, length, width), lambda j: (0, j, 0, 0)),
            pl.BlockSpec(weight.shape, lambda j: (0, 0, 0)),
        ],
        out_specs=pl.BlockSpec((1, length, cols), lambda j: (j, 0, 0)),
        out_shape=jax.ShapeDtypeStruct((count, length, cols), BF16),
        compiler_params=pltpu.CompilerParams(vmem_limit_bytes=40 << 20),
        name="project",
    )(rows, weight)


def body(
    entry_x, entry_z, entry_bc, entry_dt, source_rank, source_slot, row_spans,
    conv_x_weight, conv_x_bias, conv_bc_weight, conv_bc_bias,
    dt_bias, a_log, d_skip, norm_gain, out_weight,
):
    length, width = entry_x.shape[1:]
    ranks, groups = lax.axis_size("dp"), lax.axis_size("tensor")
    me = lax.axis_index("dp").astype(jnp.int32)
    rank = me.reshape(1)

    dt_rows = jnp.swapaxes(entry_dt, 1, 2)
    ends = jnp.concatenate([entry_x[:, length - EXTRA :], entry_bc[:, length - EXTRA :]], 2)
    tails = shifted(ends, "seq", 1)

    def packed(peer):
        peer = jnp.clip(peer, 0, ranks - 1).astype(jnp.int32)
        return pack(source_slot, peer, entry_x, entry_z, entry_bc, dt_rows, tails)

    down_main, down_gate = packed(rank - 1)
    up_main, up_gate = packed(rank + 1)
    right = shifted(down_main, "dp", -1)
    left = shifted(up_main, "dp", 1)
    own, own_gate = packed(rank)

    cols = out_weight.shape[1] // groups
    pieces = jnp.swapaxes(out_weight.reshape(width, groups, cols), 0, 1)
    weight = lax.all_to_all(pieces, "tensor", 0, 0, tiled=True)

    down_gate, up_gate, left, right = lax.optimization_barrier((down_gate, up_gate, left, right))
    right_gate = shifted(down_gate, "dp", -1)
    left_gate = shifted(up_gate, "dp", 1)

    base, scale, c_act, ended = scan(
        rank, source_rank, row_spans, dt_bias, a_log, d_skip, own, left, right,
        conv_x_weight, conv_bc_weight, conv_x_bias.reshape(1, -1), conv_bc_bias.reshape(1, -1),
    )
    carried = shifted(ended, "seq", 1)
    normed = gate(
        rank, source_rank, row_spans, base, scale, c_act, carried,
        own_gate, left_gate, right_gate, norm_gain.reshape(1, -1),
    )
    gathered = lax.all_gather(normed, "tensor", axis=0)
    return project(gathered, weight)


def solution(mesh):
    split = P("dp", "seq", "tensor")
    placed = (
        split, split, P("dp", "seq", None), split, P(), P(), P(),
        P(None, "tensor"), P("tensor"), P(), P(),
        P("tensor"), P("tensor"), P("tensor"), P("tensor"), P("tensor", None),
    )
    return jax.shard_map(body, mesh=mesh, in_specs=placed, out_specs=split, check_vma=False)
```

```python
import jax
import jax.numpy as jnp
from jax import lax
from jax.experimental import pallas as pl
from jax.experimental.pallas import tpu as pltpu
from jax.sharding import PartitionSpec as P

HEAD = 64
EXTRA = 16
EPS = 1e-05
F32 = jnp.float32
BF16 = jnp.bfloat16


def shifted(value, axis, steps):
    count = lax.axis_size(axis)
    first, last = (max(0, -steps), min(count, count - steps))
    return lax.ppermute(value, axis, [(source, source + steps) for source in range(first, last)])


MESH = pl.DeviceIdType.MESH
ANY = pl.BlockSpec(memory_space=pl.ANY)
VMEM = pl.BlockSpec(memory_space=pltpu.VMEM)
SMEM = pl.BlockSpec(memory_space=pltpu.SMEM)


def exchange_kernel(
    slot_ref, x_ref, z_ref, bc_ref, dt_ref, weight_in,
    own_ref, left_ref, right_ref, own_gate, up_gate, down_gate, weight_ref,
    tail_x, tail_bc, send, tail_send, tail_recv, move_send, move_recv, part_send, part_recv, local,
):
    ranks, pieces, groups = (lax.axis_size(axis) for axis in ("dp", "seq", "tensor"))
    d, q, m = (lax.axis_index(axis) for axis in ("dp", "seq", "tensor"))
    count = slot_ref.shape[1]
    length, width = x_ref.shape[1:]
    heads = dt_ref.shape[1]
    cols = weight_ref.shape[2]

    barrier = pltpu.get_barrier_semaphore()
    near = (
        (d > 0, {"dp": d - 1}), (d < ranks - 1, {"dp": d + 1}),
        (q > 0, {"seq": q - 1}), (q < pieces - 1, {"seq": q + 1}),
    )
    for there, target in near:
        @pl.when(there)
        def _(target=target):
            pl.semaphore_signal(barrier, inc=1, device_id=target, device_id_type=MESH)
    for k in range(1, groups):
        peer = lax.rem(m + k, groups)
        pl.semaphore_signal(barrier, inc=1, device_id={"tensor": peer}, device_id_type=MESH)
    pl.semaphore_wait(barrier, groups - 1 + sum(there.astype(jnp.int32) for there, _ in near))

    def tail_copies():
        ends = pl.ds(length - EXTRA, EXTRA)
        target = {"seq": q + 1}
        return [
            pltpu.make_async_remote_copy(
                ref.at[:, ends, :], dst, tail_send.at[i], tail_recv.at[i],
                device_id=target, device_id_type=MESH,
            )
            for i, (ref, dst) in enumerate(((x_ref, tail_x), (bc_ref, tail_bc)))
        ]

    def move(side, j):
        dst = (right_ref, left_ref)[side]
        return pltpu.make_async_remote_copy(
            send.at[side, j], dst.at[j], move_send.at[side, j], move_recv.at[side, j],
            device_id={"dp": d + (2 * side - 1)}, device_id_type=MESH,
        )

    def part(k):
        peer = lax.rem(m + k, groups)
        return pltpu.make_async_remote_copy(
            weight_in.at[:, pl.ds(pl.multiple_of(peer * cols, cols), cols)],
            weight_ref.at[m], part_send.at[k - 1], part_recv.at[k - 1],
            device_id={"tensor": peer}, device_id_type=MESH,
        )

    def arrived(k):
        peer = lax.rem(m - k + groups, groups)
        return pltpu.make_async_remote_copy(
            weight_in.at[:, pl.ds(0, cols)],
            weight_ref.at[peer], part_send.at[k - 1], part_recv.at[k - 1],
            device_id={"tensor": peer}, device_id_type=MESH,
        )

    @pl.when(q < pieces - 1)
    def _():
        for copy in tail_copies():
            copy.start()

    keep = pltpu.make_async_copy(
        weight_in.at[:, pl.ds(pl.multiple_of(m * cols, cols), cols)], weight_ref.at[m], local.at[0]
    )
    keep.start()
    for k in range(1, groups):
        part(k).start()

    @pl.when(q == 0)
    def _():
        tail_x[...] = jnp.zeros_like(tail_x)
        tail_bc[...] = jnp.zeros_like(tail_bc)

    @pl.when(q > 0)
    def _():
        for copy in tail_copies():
            copy.wait_recv()

    def fill(ref, at, slot):
        ref[at + (slice(0, length), slice(0, width))] = x_ref[slot]
        ref[at + (slice(0, length), slice(width, None))] = bc_ref[slot]
        ref[at + (slice(length, None), slice(0, width))] = tail_x[slot]
        ref[at + (slice(length, None), slice(width, None))] = tail_bc[slot]
        ref[at + (slice(length, length + heads), slice(0, length))] = dt_ref[slot]

    sides = ((d > 0, jnp.maximum(d - 1, 0)), (d < ranks - 1, jnp.minimum(d + 1, ranks - 1)))
    for j in range(count):
        for side, (there, peer) in enumerate(sides):
            fill(send, (side, j), slot_ref[peer, j])

            @pl.when(there)
            def _(side=side, j=j):
                move(side, j).start()
    for j in range(count):
        fill(own_ref, (j,), slot_ref[d, j])
        own_gate[j] = z_ref[slot_ref[d, j]]
        down_gate[j] = z_ref[slot_ref[sides[0][1], j]]
        up_gate[j] = z_ref[slot_ref[sides[1][1], j]]

    for side in range(2):
        there, back = sides[side][0], sides[1 - side][0]
        for j in range(count):
            @pl.when(there)
            def _(side=side, j=j):
                move(side, j).wait_send()

            @pl.when(back)
            def _(side=side, j=j):
                move(side, j).wait_recv()

    @pl.when(q < pieces - 1)
    def _():
        for copy in tail_copies():
            copy.wait_send()

    keep.wait()
    for k in range(1, groups):
        part(k).wait_send()
        arrived(k).wait_recv()


def exchange(source_slot, entry_x, entry_z, entry_bc, dt_rows, out_weight, groups):
    count = source_slot.shape[1]
    slots, length, width = entry_x.shape
    bc_width = entry_bc.shape[2]
    full = width + bc_width
    cols = out_weight.shape[1] // groups
    main = jax.ShapeDtypeStruct((count, length + EXTRA, full), BF16)
    small = jax.ShapeDtypeStruct((count, length, width), BF16)
    dma = pltpu.SemaphoreType.DMA
    return pl.pallas_call(
        exchange_kernel,
        in_specs=[SMEM, VMEM, VMEM, VMEM, VMEM, ANY],
        out_specs=[VMEM, ANY, ANY, VMEM, VMEM, VMEM, ANY],
        out_shape=[
            main, main, main, small, small, small,
            jax.ShapeDtypeStruct((groups, width, cols), BF16),
        ],
        scratch_shapes=[
            pltpu.VMEM((slots, EXTRA, width), BF16),
            pltpu.VMEM((slots, EXTRA, bc_width), BF16),
            pltpu.VMEM((2, count, length + EXTRA, full), BF16),
            dma((2,)), dma((2,)), dma((2, count)), dma((2, count)),
            dma((max(groups - 1, 1),)), dma((max(groups - 1, 1),)), dma((1,)),
        ],
        compiler_params=pltpu.CompilerParams(
            collective_id=0, has_side_effects=True, vmem_limit_bytes=40 << 20
        ),
        name="exchange",
    )(source_slot, entry_x, entry_z, entry_bc, dt_rows, out_weight)


def slot_row(spans_ref, rank, j, count):
    start, opens, final = jnp.int32(0), jnp.int32(0), jnp.int32(0)
    for k in range(count):
        span = spans_ref[rank, k]
        inside = (j >= start) & (j < start + span)
        opens = jnp.where(inside & (j == start), 1, opens)
        final = jnp.where(inside, start + span - 1, final)
        start = start + span
    return opens == 1, final


def choose(rank_of, rank, own, left, right):
    return jnp.where(rank_of == rank, own, jnp.where(rank_of < rank, left, right))


def scan_kernel(
    rank_ref, source_ref, spans_ref, dtb_ref, alog_ref, skip_ref,
    own_ref, left_ref, right_ref, wx_ref, wbc_ref, bx_ref, bbc_ref,
    base_ref, scale_ref, c_ref, end_ref,
    joined, tail, state, decay, mixes, spread, weighted,
):
    j = pl.program_id(0)
    rank = rank_ref[0]
    count = own_ref.shape[0]
    length = own_ref.shape[1] - EXTRA
    width = wx_ref.shape[1]
    bc_width = wbc_ref.shape[1]
    states = bc_width // 2
    taps = wx_ref.shape[0]
    heads = width // HEAD
    opens, final = slot_row(spans_ref, rank, j, count)

    def moved(slot, rows):
        parts = [ref[slot, rows, :].astype(F32) for ref in (own_ref, left_ref, right_ref)]
        return choose(source_ref[rank, slot], rank, *parts)

    before = moved(final, slice(length, length + EXTRA))[EXTRA - 8 :]
    joined[0:8, :] = jnp.where(opens, before, tail[...])
    joined[8 : 8 + length, :] = moved(j, slice(0, length))
    steps = moved(j, slice(length, length + EXTRA))[0:8, :length]
    tail[...] = joined[length : length + 8, :]

    def conv(weight_ref, bias_ref, first, last):
        total = bias_ref[...]
        for k in range(taps):
            offset = 8 - (taps - 1) + k
            total = total + weight_ref[k : k + 1, :] * joined[offset : offset + length, first:last]
        return (total / (1.0 + jnp.exp(-total))).astype(BF16)

    xc = conv(wx_ref, bx_ref, 0, width)
    bc = conv(wbc_ref, bbc_ref, width, width + bc_width)
    b_rows = jnp.transpose(bc[:, :states].astype(F32))
    c_act = bc[:, states:]
    c_ref[0] = c_act

    row = lax.broadcasted_iota(jnp.int32, (8, length), 0)
    shift = jnp.zeros((8, length), F32)
    rate = jnp.zeros((8, length), F32)
    for h in range(heads):
        shift = jnp.where(row == h, dtb_ref[h], shift)
        rate = jnp.where(row == h, alog_ref[h], rate)
    raw = steps + shift
    dt = jnp.maximum(raw, 0.0) + jnp.log1p(jnp.exp(-jnp.abs(raw)))
    rates = jnp.where(row < heads, -jnp.exp(rate) * dt, 0.0)
    t_at = lax.broadcasted_iota(jnp.int32, (length, length), 0)
    s_at = lax.broadcasted_iota(jnp.int32, (length, length), 1)
    lower = t_at >= s_at
    ones = jnp.where(lower, 1.0, 0.0).astype(BF16)
    hi = rates.astype(BF16)
    mid = (rates - hi.astype(F32)).astype(BF16)
    low = (rates - hi.astype(F32) - mid.astype(F32)).astype(BF16)
    across = (((1,), (1,)), ((), ()))
    cum_rows = sum(
        lax.dot_general(part, ones, across, preferred_element_type=F32) for part in (low, mid, hi)
    )
    padded = jnp.concatenate([cum_rows] + [jnp.zeros((120, length), F32)], 0)
    cum_cols = jnp.transpose(padded)
    total = cum_rows[:, length - 1 :]
    gone = jnp.exp(total - cum_rows) * dt

    gram = jnp.dot(c_act, b_rows.astype(BF16), preferred_element_type=F32)
    lane_head = lax.broadcasted_iota(jnp.int32, (length, width), 1) // HEAD
    cum_wide = jnp.zeros((length, width), F32)
    skip_wide = jnp.zeros((1, width), F32)
    for h in range(heads):
        column = cum_cols[:, h : h + 1]
        gap = jnp.where(lower, column - cum_rows[h : h + 1, :], -jnp.inf)
        mix = gram * jnp.exp(gap) * dt[h : h + 1, :]
        mixes[:, h * length : (h + 1) * length] = mix.astype(BF16)
        weighted[:, h * length : (h + 1) * length] = (gone[h : h + 1, :] * b_rows).astype(BF16)
        spread[h * length : (h + 1) * length, :] = jnp.where(
            lane_head == h, xc.astype(F32), 0.0
        ).astype(BF16)
        cum_wide = jnp.where(lane_head == h, column, cum_wide)
        skip_wide = jnp.where(lane_head[0:1] == h, skip_ref[h], skip_wide)
    intra = jnp.dot(mixes[...], spread[...], preferred_element_type=F32)
    contrib = jnp.dot(weighted[...], spread[...], preferred_element_type=F32)

    grown = jnp.exp(cum_wide)
    block_decay = grown[length - 1 : length, :]
    entering = jnp.where(opens, 0.0, state[...])
    passed = jnp.where(opens, 1.0, decay[...])
    ent_hi = entering.astype(BF16)
    ent_lo = (entering - ent_hi.astype(F32)).astype(BF16)
    read = jnp.dot(c_act, ent_hi, preferred_element_type=F32) + jnp.dot(
        c_act, ent_lo, preferred_element_type=F32
    )
    base_ref[0] = intra + grown * read + skip_wide * xc.astype(F32)
    scale_ref[0] = grown * passed
    ended = block_decay * entering + contrib
    state[...] = ended
    decay[...] = passed * block_decay
    end_ref[0] = ended


def scan(rank, source_rank, row_spans, dt_bias, a_log, d_skip, own, left, right, wx, wbc, bx, bbc):
    count, tall, full = own.shape
    length = tall - EXTRA
    width, bc_width = wx.shape[1], wbc.shape[1]
    heads, states = width // HEAD, bc_width // 2

    def whole(array):
        return pl.BlockSpec(array.shape, lambda j, *_: (0,) * array.ndim)

    def slot(rows, cols):
        return pl.BlockSpec((1, rows, cols), lambda j, *_: (j, 0, 0))

    return pl.pallas_call(
        scan_kernel,
        grid_spec=pltpu.PrefetchScalarGridSpec(
            num_scalar_prefetch=6,
            grid=(count,),
            in_specs=[whole(array) for array in (own, left, right, wx, wbc, bx, bbc)],
            out_specs=[
                slot(length, width), slot(length, width), slot(length, states), slot(states, width)
            ],
            scratch_shapes=[
                pltpu.VMEM((length + 8, full), F32),
                pltpu.VMEM((8, full), F32),
                pltpu.VMEM((states, width), F32),
                pltpu.VMEM((1, width), F32),
                pltpu.VMEM((length, heads * length), BF16),
                pltpu.VMEM((heads * length, width), BF16),
                pltpu.VMEM((states, heads * length), BF16),
            ],
        ),
        out_shape=[
            jax.ShapeDtypeStruct((count, length, width), F32),
            jax.ShapeDtypeStruct((count, length, width), F32),
            jax.ShapeDtypeStruct((count, length, states), BF16),
            jax.ShapeDtypeStruct((count, states, width), F32),
        ],
        compiler_params=pltpu.CompilerParams(vmem_limit_bytes=40 << 20),
        cost_estimate=pl.CostEstimate(
            flops=3_000_000_000, bytes_accessed=8_000_000, transcendentals=2_000_000
        ),
        name="scan",
    )(rank, source_rank, row_spans, dt_bias, a_log, d_skip, own, left, right, wx, wbc, bx, bbc)


def finish_kernel(
    rank_ref, source_ref, spans_ref,
    base_ref, scale_ref, c_ref, carried_ref, own_ref, left_ref, right_ref, gain_ref, weight_ref,
    out_ref, rows, right_send, left_send, arrive,
):
    groups = weight_ref.shape[0]
    count = base_ref.shape[0]
    rank = rank_ref[0]
    m = lax.axis_index("tensor")
    barrier = pltpu.get_barrier_semaphore()
    near = ((m > 0, m - 1), (m < groups - 1, m + 1))
    for there, peer in near:
        @pl.when(there)
        def _(peer=peer):
            pl.semaphore_signal(barrier, inc=1, device_id={"tensor": peer}, device_id_type=MESH)
    pl.semaphore_wait(barrier, sum(there.astype(jnp.int32) for there, _ in near))

    def hop(side, source, j):
        return pltpu.make_async_remote_copy(
            rows.at[source, j], rows.at[source, j],
            (left_send, right_send)[side].at[source, j], arrive.at[source, j],
            device_id={"tensor": m + (2 * side - 1)}, device_id_type=MESH,
        )

    for j in range(count):
        _, final = slot_row(spans_ref, rank, jnp.int32(j), count)
        carried = carried_ref[final]
        high = carried.astype(BF16)
        low = (carried - high.astype(F32)).astype(BF16)
        c_act = c_ref[j]
        read = jnp.dot(c_act, high, preferred_element_type=F32) + jnp.dot(
            c_act, low, preferred_element_type=F32
        )
        y = base_ref[j] + scale_ref[j] * read
        parts = [ref[j].astype(F32) for ref in (own_ref, left_ref, right_ref)]
        z = choose(source_ref[rank, j], rank, *parts)
        g = y * (z / (1.0 + jnp.exp(-z)))
        inverse = lax.rsqrt(jnp.mean(g * g, axis=-1, keepdims=True) + EPS)
        rows[m, j] = (g * inverse * gain_ref[...]).astype(BF16)
        for side, (there, _) in enumerate(near):
            @pl.when(there)
            def _(side=side, j=j):
                hop(side, m, j).start()

    def one_slot(j, token):
        for k in range(1, groups):
            for side in range(2):
                source = m - k if side == 1 else m + k
                here = (source >= 0) if side == 1 else (source < groups)

                @pl.when(here)
                def _(side=side, source=source):
                    hop(side, source, j).wait_recv()

                @pl.when(here & near[side][0])
                def _(side=side, source=source):
                    hop(side, source, j).start()
        total = jnp.dot(rows[0, j], weight_ref[0], preferred_element_type=F32)
        for i in range(1, groups):
            total = total + jnp.dot(rows[i, j], weight_ref[i], preferred_element_type=F32)
        out_ref[j] = total.astype(BF16)
        return token

    lax.fori_loop(0, count, one_slot, 0)

    def drain(j, token):
        for side, (there, _) in enumerate(near):
            @pl.when(there)
            def _(side=side):
                hop(side, m, j).wait_send()
        for k in range(1, groups):
            for side in range(2):
                source = m - k if side == 1 else m + k
                here = (source >= 0) if side == 1 else (source < groups)

                @pl.when(here & near[side][0])
                def _(side=side, source=source):
                    hop(side, source, j).wait_send()
        return token

    lax.fori_loop(0, count, drain, 0)


def finish(
    rank, source_rank, row_spans, base, scale, c_act, carried, own, left, right, gain, weight
):
    count, length, width = base.shape
    groups, _, cols = weight.shape
    dma = pltpu.SemaphoreType.DMA
    return pl.pallas_call(
        finish_kernel,
        in_specs=[SMEM] * 3 + [VMEM] * 9,
        out_specs=VMEM,
        out_shape=jax.ShapeDtypeStruct((count, length, cols), BF16),
        scratch_shapes=[
            pltpu.VMEM((groups, count, length, width), BF16),
            dma((groups, count)), dma((groups, count)), dma((groups, count)),
        ],
        compiler_params=pltpu.CompilerParams(
            collective_id=1, has_side_effects=True, vmem_limit_bytes=48 << 20
        ),
        name="finish",
    )(rank, source_rank, row_spans, base, scale, c_act, carried, own, left, right, gain, weight)


def body(
    entry_x, entry_z, entry_bc, entry_dt, source_rank, source_slot, row_spans,
    conv_x_weight, conv_x_bias, conv_bc_weight, conv_bc_bias,
    dt_bias, a_log, d_skip, norm_gain, out_weight,
):
    groups = lax.axis_size("tensor")
    me = lax.axis_index("dp").astype(jnp.int32)
    rank = me.reshape(1)

    dt_rows = jnp.swapaxes(entry_dt, 1, 2)
    own, left, right, own_gate, up_gate, down_gate, weight = exchange(
        source_slot, entry_x, entry_z, entry_bc, dt_rows, out_weight, groups
    )
    right_gate = shifted(down_gate, "dp", -1)
    left_gate = shifted(up_gate, "dp", 1)

    base, scale, c_act, ended = scan(
        rank, source_rank, row_spans, dt_bias, a_log, d_skip, own, left, right,
        conv_x_weight, conv_bc_weight, conv_x_bias.reshape(1, -1), conv_bc_bias.reshape(1, -1),
    )
    carried = shifted(ended, "seq", 1)
    return finish(
        rank, source_rank, row_spans, base, scale, c_act, carried,
        own_gate, left_gate, right_gate, norm_gain.reshape(1, -1), weight,
    )


def solution(mesh):
    split = P("dp", "seq", "tensor")
    placed = (
        split, split, P("dp", "seq", None), split, P(), P(), P(),
        P(None, "tensor"), P("tensor"), P(), P(),
        P("tensor"), P("tensor"), P("tensor"), P("tensor"), P("tensor", None),
    )
    return jax.shard_map(body, mesh=mesh, in_specs=placed, out_specs=split, check_vma=False)
```

```python
import jax
import jax.numpy as jnp
from jax import lax
from jax.experimental import pallas as pl
from jax.experimental.pallas import tpu as pltpu
from jax.sharding import PartitionSpec as P

HEAD = 64
EXTRA = 16
EPS = 1e-05
F32 = jnp.float32
BF16 = jnp.bfloat16


MESH = pl.DeviceIdType.MESH
ANY = pl.BlockSpec(memory_space=pl.ANY)
VMEM = pl.BlockSpec(memory_space=pltpu.VMEM)
SMEM = pl.BlockSpec(memory_space=pltpu.SMEM)


def slot_row(spans_ref, rank, j, count):
    start, opens, final = jnp.int32(0), jnp.int32(0), jnp.int32(0)
    for k in range(count):
        span = spans_ref[rank, k]
        inside = (j >= start) & (j < start + span)
        opens = jnp.where(inside & (j == start), 1, opens)
        final = jnp.where(inside, start + span - 1, final)
        start = start + span
    return opens == 1, final


def choose(rank_of, rank, own, left, right):
    return jnp.where(rank_of == rank, own, jnp.where(rank_of < rank, left, right))


def scan_slot(
    j, rank, source_ref, spans_ref, dtb_ref, alog_ref, skip_ref,
    own_ref, left_ref, right_ref, wx_ref, wbc_ref, bx_ref, bbc_ref,
    base_ref, scale_ref, c_ref, end_ref,
    joined, tail, state, decay, mixes, spread, weighted,
):
    count = own_ref.shape[0]
    length = own_ref.shape[1] - EXTRA
    width = wx_ref.shape[1]
    bc_width = wbc_ref.shape[1]
    states = bc_width // 2
    taps = wx_ref.shape[0]
    heads = width // HEAD
    opens, final = slot_row(spans_ref, rank, j, count)

    def moved(slot, rows):
        parts = [ref[slot, rows, :].astype(F32) for ref in (own_ref, left_ref, right_ref)]
        return choose(source_ref[rank, slot], rank, *parts)

    before = moved(final, slice(length, length + EXTRA))[EXTRA - 8 :]
    joined[0:8, :] = jnp.where(opens, before, tail[...])
    joined[8 : 8 + length, :] = moved(j, slice(0, length))
    steps = moved(j, slice(length, length + EXTRA))[0:8, :length]
    tail[...] = joined[length : length + 8, :]

    def conv(weight_ref, bias_ref, first, last):
        total = bias_ref[...]
        for k in range(taps):
            offset = 8 - (taps - 1) + k
            total = total + weight_ref[k : k + 1, :] * joined[offset : offset + length, first:last]
        return (total / (1.0 + jnp.exp(-total))).astype(BF16)

    xc = conv(wx_ref, bx_ref, 0, width)
    bc = conv(wbc_ref, bbc_ref, width, width + bc_width)
    b_rows = jnp.transpose(bc[:, :states].astype(F32))
    c_act = bc[:, states:]
    c_ref[j] = c_act

    row = lax.broadcasted_iota(jnp.int32, (8, length), 0)
    shift = jnp.zeros((8, length), F32)
    rate = jnp.zeros((8, length), F32)
    for h in range(heads):
        shift = jnp.where(row == h, dtb_ref[h], shift)
        rate = jnp.where(row == h, alog_ref[h], rate)
    raw = steps + shift
    dt = jnp.maximum(raw, 0.0) + jnp.log1p(jnp.exp(-jnp.abs(raw)))
    rates = jnp.where(row < heads, -jnp.exp(rate) * dt, 0.0)
    t_at = lax.broadcasted_iota(jnp.int32, (length, length), 0)
    s_at = lax.broadcasted_iota(jnp.int32, (length, length), 1)
    lower = t_at >= s_at
    ones = jnp.where(lower, 1.0, 0.0).astype(BF16)
    hi = rates.astype(BF16)
    mid = (rates - hi.astype(F32)).astype(BF16)
    low = (rates - hi.astype(F32) - mid.astype(F32)).astype(BF16)
    across = (((1,), (1,)), ((), ()))
    cum_rows = sum(
        lax.dot_general(part, ones, across, preferred_element_type=F32) for part in (low, mid, hi)
    )
    padded = jnp.concatenate([cum_rows] + [jnp.zeros((120, length), F32)], 0)
    cum_cols = jnp.transpose(padded)
    total = cum_rows[:, length - 1 :]
    gone = jnp.exp(total - cum_rows) * dt

    gram = jnp.dot(c_act, b_rows.astype(BF16), preferred_element_type=F32)
    lane_head = lax.broadcasted_iota(jnp.int32, (length, width), 1) // HEAD
    cum_wide = jnp.zeros((length, width), F32)
    skip_wide = jnp.zeros((1, width), F32)
    for h in range(heads):
        column = cum_cols[:, h : h + 1]
        gap = jnp.where(lower, column - cum_rows[h : h + 1, :], -jnp.inf)
        mix = gram * jnp.exp(gap) * dt[h : h + 1, :]
        mixes[:, h * length : (h + 1) * length] = mix.astype(BF16)
        weighted[:, h * length : (h + 1) * length] = (gone[h : h + 1, :] * b_rows).astype(BF16)
        spread[h * length : (h + 1) * length, :] = jnp.where(
            lane_head == h, xc.astype(F32), 0.0
        ).astype(BF16)
        cum_wide = jnp.where(lane_head == h, column, cum_wide)
        skip_wide = jnp.where(lane_head[0:1] == h, skip_ref[h], skip_wide)
    intra = jnp.dot(mixes[...], spread[...], preferred_element_type=F32)
    contrib = jnp.dot(weighted[...], spread[...], preferred_element_type=F32)

    grown = jnp.exp(cum_wide)
    block_decay = grown[length - 1 : length, :]
    entering = jnp.where(opens, 0.0, state[...])
    passed = jnp.where(opens, 1.0, decay[...])
    ent_hi = entering.astype(BF16)
    ent_lo = (entering - ent_hi.astype(F32)).astype(BF16)
    read = jnp.dot(c_act, ent_hi, preferred_element_type=F32) + jnp.dot(
        c_act, ent_lo, preferred_element_type=F32
    )
    base_ref[j] = intra + grown * read + skip_wide * xc.astype(F32)
    scale_ref[j] = grown * passed
    ended = block_decay * entering + contrib
    state[...] = ended
    decay[...] = passed * block_decay
    end_ref[j] = ended


def mixer_kernel(
    slot_ref, source_ref, spans_ref, dtb_ref, alog_ref, skip_ref,
    x_ref, z_ref, bc_ref, dt_ref, wx_ref, wbc_ref, bx_ref, bbc_ref, gain_ref, weight_in,
    out_ref,
    own_ref, left_ref, right_ref, own_gate, left_gate, right_gate, gate_send, weight_ref,
    tail_x, tail_bc, send, base_ref, scale_ref, c_ref, end_ref, carried_ref, rows,
    joined, tail, state, decay, mixes, spread, weighted,
    tail_send, tail_recv, move_send, move_recv, gate_sent, gate_came, part_send, part_recv, local,
    state_send, state_recv, right_send, left_send, arrive,
):
    ranks, pieces, groups = (lax.axis_size(axis) for axis in ("dp", "seq", "tensor"))
    d, q, m = (lax.axis_index(axis) for axis in ("dp", "seq", "tensor"))
    count = slot_ref.shape[1]
    length, width = x_ref.shape[1:]
    heads = dt_ref.shape[1]
    cols = weight_ref.shape[2]

    barrier = pltpu.get_barrier_semaphore()
    near = (
        (d > 0, {"dp": d - 1}), (d < ranks - 1, {"dp": d + 1}),
        (q > 0, {"seq": q - 1}), (q < pieces - 1, {"seq": q + 1}),
    )
    for there, target in near:
        @pl.when(there)
        def _(target=target):
            pl.semaphore_signal(barrier, inc=1, device_id=target, device_id_type=MESH)
    for k in range(1, groups):
        peer = lax.rem(m + k, groups)
        pl.semaphore_signal(barrier, inc=1, device_id={"tensor": peer}, device_id_type=MESH)
    pl.semaphore_wait(barrier, groups - 1 + sum(there.astype(jnp.int32) for there, _ in near))

    def tail_copies():
        ends = pl.ds(length - EXTRA, EXTRA)
        target = {"seq": q + 1}
        return [
            pltpu.make_async_remote_copy(
                ref.at[:, ends, :], dst, tail_send.at[i], tail_recv.at[i],
                device_id=target, device_id_type=MESH,
            )
            for i, (ref, dst) in enumerate(((x_ref, tail_x), (bc_ref, tail_bc)))
        ]

    def move(side, j):
        dst = (right_ref, left_ref)[side]
        return pltpu.make_async_remote_copy(
            send.at[side, j], dst.at[j], move_send.at[side, j], move_recv.at[side, j],
            device_id={"dp": d + (2 * side - 1)}, device_id_type=MESH,
        )

    def part(k):
        peer = lax.rem(m + k, groups)
        return pltpu.make_async_remote_copy(
            weight_in.at[:, pl.ds(pl.multiple_of(peer * cols, cols), cols)],
            weight_ref.at[m], part_send.at[k - 1], part_recv.at[k - 1],
            device_id={"tensor": peer}, device_id_type=MESH,
        )

    def arrived(k):
        peer = lax.rem(m - k + groups, groups)
        return pltpu.make_async_remote_copy(
            weight_in.at[:, pl.ds(0, cols)],
            weight_ref.at[peer], part_send.at[k - 1], part_recv.at[k - 1],
            device_id={"tensor": peer}, device_id_type=MESH,
        )

    @pl.when(q < pieces - 1)
    def _():
        for copy in tail_copies():
            copy.start()

    keep = pltpu.make_async_copy(
        weight_in.at[:, pl.ds(pl.multiple_of(m * cols, cols), cols)], weight_ref.at[m], local.at[0]
    )
    keep.start()
    for k in range(1, groups):
        part(k).start()

    @pl.when(q == 0)
    def _():
        tail_x[...] = jnp.zeros_like(tail_x)
        tail_bc[...] = jnp.zeros_like(tail_bc)

    @pl.when(q > 0)
    def _():
        for copy in tail_copies():
            copy.wait_recv()

    def fill(ref, at, slot):
        ref[at + (slice(0, length), slice(0, width))] = x_ref[slot]
        ref[at + (slice(0, length), slice(width, None))] = bc_ref[slot]
        ref[at + (slice(length, None), slice(0, width))] = tail_x[slot]
        ref[at + (slice(length, None), slice(width, None))] = tail_bc[slot]
        ref[at + (slice(length, length + heads), slice(0, length))] = dt_ref[slot]

    sides = ((d > 0, jnp.maximum(d - 1, 0)), (d < ranks - 1, jnp.minimum(d + 1, ranks - 1)))
    for j in range(count):
        for side, (there, peer) in enumerate(sides):
            fill(send, (side, j), slot_ref[peer, j])

            @pl.when(there)
            def _(side=side, j=j):
                move(side, j).start()
    for j in range(count):
        fill(own_ref, (j,), slot_ref[d, j])
        own_gate[j] = z_ref[slot_ref[d, j]]
        gate_send[0, j] = z_ref[slot_ref[sides[0][1], j]]
        gate_send[1, j] = z_ref[slot_ref[sides[1][1], j]]

    def move_gate(side):
        dst = (right_gate, left_gate)[side]
        return pltpu.make_async_remote_copy(
            gate_send.at[side], dst, gate_sent.at[side], gate_came.at[side],
            device_id={"dp": d + (2 * side - 1)}, device_id_type=MESH,
        )

    for side in range(2):
        @pl.when(sides[side][0])
        def _(side=side):
            for j in range(count):
                move(side, j).wait_send()
            move_gate(side).start()

    for side in range(2):
        @pl.when(sides[1 - side][0])
        def _(side=side):
            for j in range(count):
                move(side, j).wait_recv()

    def scan_step(j, token):
        scan_slot(
            j, d, source_ref, spans_ref, dtb_ref, alog_ref, skip_ref,
            own_ref, left_ref, right_ref, wx_ref, wbc_ref, bx_ref, bbc_ref,
            base_ref, scale_ref, c_ref, end_ref,
            joined, tail, state, decay, mixes, spread, weighted,
        )
        return token

    lax.fori_loop(0, count, scan_step, 0)

    hand = pltpu.make_async_remote_copy(
        end_ref, carried_ref, state_send.at[0], state_recv.at[0],
        device_id={"seq": q + 1}, device_id_type=MESH,
    )

    @pl.when(q < pieces - 1)
    def _():
        hand.start()

    @pl.when(q == 0)
    def _():
        carried_ref[...] = jnp.zeros_like(carried_ref)

    @pl.when(q > 0)
    def _():
        hand.wait_recv()

    for side in range(2):
        @pl.when(sides[1 - side][0])
        def _(side=side):
            move_gate(side).wait_recv()

    beside = ((m > 0, m - 1), (m < groups - 1, m + 1))

    def hop(side, source, j):
        return pltpu.make_async_remote_copy(
            rows.at[source, j], rows.at[source, j],
            (left_send, right_send)[side].at[source, j], arrive.at[source, j],
            device_id={"tensor": m + (2 * side - 1)}, device_id_type=MESH,
        )

    for j in range(count):
        _, final = slot_row(spans_ref, d, jnp.int32(j), count)
        carried = carried_ref[final]
        high = carried.astype(BF16)
        low = (carried - high.astype(F32)).astype(BF16)
        c_act = c_ref[j]
        read = jnp.dot(c_act, high, preferred_element_type=F32) + jnp.dot(
            c_act, low, preferred_element_type=F32
        )
        y = base_ref[j] + scale_ref[j] * read
        parts = [ref[j].astype(F32) for ref in (own_gate, left_gate, right_gate)]
        z = choose(source_ref[d, j], d, *parts)
        g = y * (z / (1.0 + jnp.exp(-z)))
        inverse = lax.rsqrt(jnp.mean(g * g, axis=-1, keepdims=True) + EPS)
        rows[m, j] = (g * inverse * gain_ref[...]).astype(BF16)
        for side, (there, _) in enumerate(beside):
            @pl.when(there)
            def _(side=side, j=j):
                hop(side, m, j).start()

    keep.wait()
    for k in range(1, groups):
        arrived(k).wait_recv()

    def one_slot(j, token):
        for k in range(1, groups):
            for side in range(2):
                source = m - k if side == 1 else m + k
                here = (source >= 0) if side == 1 else (source < groups)

                @pl.when(here)
                def _(side=side, source=source):
                    hop(side, source, j).wait_recv()

                @pl.when(here & beside[side][0])
                def _(side=side, source=source):
                    hop(side, source, j).start()
        total = jnp.dot(rows[0, j], weight_ref[0], preferred_element_type=F32)
        for i in range(1, groups):
            total = total + jnp.dot(rows[i, j], weight_ref[i], preferred_element_type=F32)
        out_ref[j] = total.astype(BF16)
        return token

    lax.fori_loop(0, count, one_slot, 0)

    def drain(j, token):
        for side, (there, _) in enumerate(beside):
            @pl.when(there)
            def _(side=side):
                hop(side, m, j).wait_send()
        for k in range(1, groups):
            for side in range(2):
                source = m - k if side == 1 else m + k
                here = (source >= 0) if side == 1 else (source < groups)

                @pl.when(here & beside[side][0])
                def _(side=side, source=source):
                    hop(side, source, j).wait_send()
        return token

    lax.fori_loop(0, count, drain, 0)

    for side in range(2):
        @pl.when(sides[side][0])
        def _(side=side):
            move_gate(side).wait_send()

    @pl.when(q < pieces - 1)
    def _():
        for copy in tail_copies():
            copy.wait_send()
        hand.wait_send()

    for k in range(1, groups):
        part(k).wait_send()


def body(
    entry_x, entry_z, entry_bc, entry_dt, source_rank, source_slot, row_spans,
    conv_x_weight, conv_x_bias, conv_bc_weight, conv_bc_bias,
    dt_bias, a_log, d_skip, norm_gain, out_weight,
):
    groups = lax.axis_size("tensor")
    count = source_slot.shape[1]
    slots, length, width = entry_x.shape
    bc_width = entry_bc.shape[2]
    full = width + bc_width
    heads, states = width // HEAD, bc_width // 2
    cols = out_weight.shape[1] // groups
    parts = max(groups - 1, 1)
    dma = pltpu.SemaphoreType.DMA
    main = pltpu.VMEM((count, length + EXTRA, full), BF16)
    gates = pltpu.VMEM((count, length, width), BF16)
    wide = pltpu.VMEM((count, length, width), F32)
    carry = pltpu.VMEM((count, states, width), F32)
    return pl.pallas_call(
        mixer_kernel,
        in_specs=[SMEM] * 6 + [VMEM] * 9 + [ANY],
        out_specs=VMEM,
        out_shape=jax.ShapeDtypeStruct((count, length, cols), BF16),
        scratch_shapes=[
            main, main, main, gates, gates, gates,
            pltpu.VMEM((2, count, length, width), BF16),
            pltpu.VMEM((groups, width, cols), BF16),
            pltpu.VMEM((slots, EXTRA, width), BF16),
            pltpu.VMEM((slots, EXTRA, bc_width), BF16),
            pltpu.VMEM((2, count, length + EXTRA, full), BF16),
            wide, wide, pltpu.VMEM((count, length, states), BF16), carry, carry,
            pltpu.VMEM((groups, count, length, width), BF16),
            pltpu.VMEM((length + 8, full), F32),
            pltpu.VMEM((8, full), F32),
            pltpu.VMEM((states, width), F32),
            pltpu.VMEM((1, width), F32),
            pltpu.VMEM((length, heads * length), BF16),
            pltpu.VMEM((heads * length, width), BF16),
            pltpu.VMEM((states, heads * length), BF16),
            dma((2,)), dma((2,)), dma((2, count)), dma((2, count)), dma((2,)), dma((2,)),
            dma((parts,)), dma((parts,)), dma((1,)), dma((1,)), dma((1,)),
            dma((groups, count)), dma((groups, count)), dma((groups, count)),
        ],
        compiler_params=pltpu.CompilerParams(
            collective_id=0, has_side_effects=True, vmem_limit_bytes=58 << 20
        ),
        name="mixer",
    )(
        source_slot, source_rank, row_spans, dt_bias, a_log, d_skip,
        entry_x, entry_z, entry_bc, jnp.swapaxes(entry_dt, 1, 2),
        conv_x_weight, conv_bc_weight, conv_x_bias.reshape(1, -1), conv_bc_bias.reshape(1, -1),
        norm_gain.reshape(1, -1), out_weight,
    )


def solution(mesh):
    split = P("dp", "seq", "tensor")
    placed = (
        split, split, P("dp", "seq", None), split, P(), P(), P(),
        P(None, "tensor"), P("tensor"), P(), P(),
        P("tensor"), P("tensor"), P("tensor"), P("tensor"), P("tensor", None),
    )
    return jax.shard_map(body, mesh=mesh, in_specs=placed, out_specs=split, check_vma=False)
```

```python
import jax
import jax.numpy as jnp
from jax import lax
from jax.experimental import pallas as pl
from jax.experimental.pallas import tpu as pltpu
from jax.sharding import PartitionSpec as P

HEAD = 64
EXTRA = 16
EPS = 1e-05
F32 = jnp.float32
BF16 = jnp.bfloat16


MESH = pl.DeviceIdType.MESH
ANY = pl.BlockSpec(memory_space=pl.ANY)
VMEM = pl.BlockSpec(memory_space=pltpu.VMEM)
SMEM = pl.BlockSpec(memory_space=pltpu.SMEM)


def slot_row(spans_ref, rank, j, count):
    start, opens, final = jnp.int32(0), jnp.int32(0), jnp.int32(0)
    for k in range(count):
        span = spans_ref[rank, k]
        inside = (j >= start) & (j < start + span)
        opens = jnp.where(inside & (j == start), 1, opens)
        final = jnp.where(inside, start + span - 1, final)
        start = start + span
    return opens == 1, final


def choose(rank_of, rank, own, left, right):
    return jnp.where(rank_of == rank, own, jnp.where(rank_of < rank, left, right))


def scan_slot(
    j, rank, source_ref, spans_ref, dtb_ref, alog_ref, skip_ref,
    own_ref, left_ref, right_ref, own_ends, left_ends, right_ends,
    wx_ref, wbc_ref, bx_ref, bbc_ref,
    base_ref, scale_ref, c_ref, end_ref,
    joined, tail, state, decay, mixes, spread, weighted,
):
    count = own_ref.shape[0]
    length = own_ref.shape[1]
    width = wx_ref.shape[1]
    bc_width = wbc_ref.shape[1]
    states = bc_width // 2
    taps = wx_ref.shape[0]
    heads = width // HEAD
    opens, final = slot_row(spans_ref, rank, j, count)

    def moved(slot, *refs):
        parts = [ref[slot].astype(F32) for ref in refs]
        return choose(source_ref[rank, slot], rank, *parts)

    before = moved(final, own_ends, left_ends, right_ends)[EXTRA - 8 :]
    joined[0:8, :] = jnp.where(opens, before, tail[...])
    joined[8 : 8 + length, :] = moved(j, own_ref, left_ref, right_ref)
    steps = moved(j, own_ends, left_ends, right_ends)[0:8, :length]
    tail[...] = joined[length : length + 8, :]

    def conv(weight_ref, bias_ref, first, last):
        total = bias_ref[...]
        for k in range(taps):
            offset = 8 - (taps - 1) + k
            total = total + weight_ref[k : k + 1, :] * joined[offset : offset + length, first:last]
        return (total / (1.0 + jnp.exp(-total))).astype(BF16)

    xc = conv(wx_ref, bx_ref, 0, width)
    bc = conv(wbc_ref, bbc_ref, width, width + bc_width)
    b_rows = jnp.transpose(bc[:, :states].astype(F32))
    c_act = bc[:, states:]
    c_ref[j] = c_act

    row = lax.broadcasted_iota(jnp.int32, (8, length), 0)
    shift = jnp.zeros((8, length), F32)
    rate = jnp.zeros((8, length), F32)
    for h in range(heads):
        shift = jnp.where(row == h, dtb_ref[h], shift)
        rate = jnp.where(row == h, alog_ref[h], rate)
    raw = steps + shift
    dt = jnp.maximum(raw, 0.0) + jnp.log1p(jnp.exp(-jnp.abs(raw)))
    rates = jnp.where(row < heads, -jnp.exp(rate) * dt, 0.0)
    t_at = lax.broadcasted_iota(jnp.int32, (length, length), 0)
    s_at = lax.broadcasted_iota(jnp.int32, (length, length), 1)
    lower = t_at >= s_at
    ones = jnp.where(lower, 1.0, 0.0).astype(BF16)
    hi = rates.astype(BF16)
    mid = (rates - hi.astype(F32)).astype(BF16)
    low = (rates - hi.astype(F32) - mid.astype(F32)).astype(BF16)
    across = (((1,), (1,)), ((), ()))
    cum_rows = sum(
        lax.dot_general(part, ones, across, preferred_element_type=F32) for part in (low, mid, hi)
    )
    padded = jnp.concatenate([cum_rows] + [jnp.zeros((120, length), F32)], 0)
    cum_cols = jnp.transpose(padded)
    total = cum_rows[:, length - 1 :]
    gone = jnp.exp(total - cum_rows) * dt

    gram = jnp.dot(c_act, b_rows.astype(BF16), preferred_element_type=F32)
    lane_head = lax.broadcasted_iota(jnp.int32, (length, width), 1) // HEAD
    cum_wide = jnp.zeros((length, width), F32)
    skip_wide = jnp.zeros((1, width), F32)
    for h in range(heads):
        column = cum_cols[:, h : h + 1]
        gap = jnp.where(lower, column - cum_rows[h : h + 1, :], -jnp.inf)
        mix = gram * jnp.exp(gap) * dt[h : h + 1, :]
        mixes[:, h * length : (h + 1) * length] = mix.astype(BF16)
        weighted[:, h * length : (h + 1) * length] = (gone[h : h + 1, :] * b_rows).astype(BF16)
        spread[h * length : (h + 1) * length, :] = jnp.where(
            lane_head == h, xc.astype(F32), 0.0
        ).astype(BF16)
        cum_wide = jnp.where(lane_head == h, column, cum_wide)
        skip_wide = jnp.where(lane_head[0:1] == h, skip_ref[h], skip_wide)
    intra = jnp.dot(mixes[...], spread[...], preferred_element_type=F32)
    contrib = jnp.dot(weighted[...], spread[...], preferred_element_type=F32)

    grown = jnp.exp(cum_wide)
    block_decay = grown[length - 1 : length, :]
    entering = jnp.where(opens, 0.0, state[...])
    passed = jnp.where(opens, 1.0, decay[...])
    ent_hi = entering.astype(BF16)
    ent_lo = (entering - ent_hi.astype(F32)).astype(BF16)
    read = jnp.dot(c_act, ent_hi, preferred_element_type=F32) + jnp.dot(
        c_act, ent_lo, preferred_element_type=F32
    )
    base_ref[j] = intra + grown * read + skip_wide * xc.astype(F32)
    scale_ref[j] = grown * passed
    ended = block_decay * entering + contrib
    state[...] = ended
    decay[...] = passed * block_decay
    end_ref[j] = ended


def mixer_kernel(
    slot_ref, source_ref, spans_ref, dtb_ref, alog_ref, skip_ref,
    x_ref, z_ref, bc_ref, dt_ref, wx_ref, wbc_ref, bx_ref, bbc_ref, gain_ref, weight_in,
    out_ref,
    own_ref, left_ref, right_ref, own_ends, left_ends, right_ends, send_ends,
    own_gate, left_gate, right_gate, gate_send, weight_ref,
    tail_x, tail_bc, send, base_ref, scale_ref, c_ref, end_ref, carried_ref, rows,
    joined, tail, state, decay, mixes, spread, weighted,
    tail_send, tail_recv, move_send, move_recv, gate_sent, gate_came, part_send, part_recv, local,
    state_send, state_recv, right_send, left_send, arrive, ends_send, ends_recv,
):
    ranks, pieces, groups = (lax.axis_size(axis) for axis in ("dp", "seq", "tensor"))
    d, q, m = (lax.axis_index(axis) for axis in ("dp", "seq", "tensor"))
    count = slot_ref.shape[1]
    length, width = x_ref.shape[1:]
    heads = dt_ref.shape[1]
    cols = weight_ref.shape[2]

    barrier = pltpu.get_barrier_semaphore()
    near = (
        (d > 0, {"dp": d - 1}), (d < ranks - 1, {"dp": d + 1}),
        (q > 0, {"seq": q - 1}), (q < pieces - 1, {"seq": q + 1}),
    )
    for there, target in near:
        @pl.when(there)
        def _(target=target):
            pl.semaphore_signal(barrier, inc=1, device_id=target, device_id_type=MESH)
    for k in range(1, groups):
        peer = lax.rem(m + k, groups)
        pl.semaphore_signal(barrier, inc=1, device_id={"tensor": peer}, device_id_type=MESH)
    pl.semaphore_wait(barrier, groups - 1 + sum(there.astype(jnp.int32) for there, _ in near))

    def tail_copies():
        ends = pl.ds(length - EXTRA, EXTRA)
        target = {"seq": q + 1}
        return [
            pltpu.make_async_remote_copy(
                ref.at[:, ends, :], dst, tail_send.at[i], tail_recv.at[i],
                device_id=target, device_id_type=MESH,
            )
            for i, (ref, dst) in enumerate(((x_ref, tail_x), (bc_ref, tail_bc)))
        ]

    def move(side, j):
        dst = (right_ref, left_ref)[side]
        return pltpu.make_async_remote_copy(
            send.at[side, j], dst.at[j], move_send.at[side, j], move_recv.at[side, j],
            device_id={"dp": d + (2 * side - 1)}, device_id_type=MESH,
        )

    def move_ends(side):
        dst = (right_ends, left_ends)[side]
        return pltpu.make_async_remote_copy(
            send_ends.at[side], dst, ends_send.at[side], ends_recv.at[side],
            device_id={"dp": d + (2 * side - 1)}, device_id_type=MESH,
        )

    def part(k):
        peer = lax.rem(m + k, groups)
        return pltpu.make_async_remote_copy(
            weight_in.at[:, pl.ds(pl.multiple_of(peer * cols, cols), cols)],
            weight_ref.at[m], part_send.at[k - 1], part_recv.at[k - 1],
            device_id={"tensor": peer}, device_id_type=MESH,
        )

    def arrived(k):
        peer = lax.rem(m - k + groups, groups)
        return pltpu.make_async_remote_copy(
            weight_in.at[:, pl.ds(0, cols)],
            weight_ref.at[peer], part_send.at[k - 1], part_recv.at[k - 1],
            device_id={"tensor": peer}, device_id_type=MESH,
        )

    @pl.when(q < pieces - 1)
    def _():
        for copy in tail_copies():
            copy.start()

    keep = pltpu.make_async_copy(
        weight_in.at[:, pl.ds(pl.multiple_of(m * cols, cols), cols)], weight_ref.at[m], local.at[0]
    )
    keep.start()
    for k in range(1, groups):
        part(k).start()

    def fill(ref, at, slot):
        ref[at + (slice(None), slice(0, width))] = x_ref[slot]
        ref[at + (slice(None), slice(width, None))] = bc_ref[slot]

    def fill_ends(ref, at, slot):
        ref[at + (slice(None), slice(0, width))] = tail_x[slot]
        ref[at + (slice(None), slice(width, None))] = tail_bc[slot]
        ref[at + (slice(0, heads), slice(0, length))] = dt_ref[slot]

    sides = ((d > 0, jnp.maximum(d - 1, 0)), (d < ranks - 1, jnp.minimum(d + 1, ranks - 1)))
    def send_slot(j):
        for side, (there, peer) in enumerate(sides):
            fill(send, (side, j), slot_ref[peer, j])

            @pl.when(there)
            def _(side=side):
                move(side, j).start()

    send_slot(0)

    @pl.when(q == 0)
    def _():
        tail_x[...] = jnp.zeros_like(tail_x)
        tail_bc[...] = jnp.zeros_like(tail_bc)

    @pl.when(q > 0)
    def _():
        for copy in tail_copies():
            copy.wait_recv()

    for side, (there, peer) in enumerate(sides):
        for j in range(count):
            fill_ends(send_ends, (side, j), slot_ref[peer, j])

        @pl.when(there)
        def _(side=side):
            move_ends(side).start()
    for j in range(1, count):
        send_slot(j)
    for j in range(count):
        fill(own_ref, (j,), slot_ref[d, j])
        fill_ends(own_ends, (j,), slot_ref[d, j])
        own_gate[j] = z_ref[slot_ref[d, j]]
        gate_send[0, j] = z_ref[slot_ref[sides[0][1], j]]
        gate_send[1, j] = z_ref[slot_ref[sides[1][1], j]]

    def move_gate(side, j):
        dst = (right_gate, left_gate)[side]
        return pltpu.make_async_remote_copy(
            gate_send.at[side, j], dst.at[j], gate_sent.at[side, j], gate_came.at[side, j],
            device_id={"dp": d + (2 * side - 1)}, device_id_type=MESH,
        )

    for side in range(2):
        @pl.when(sides[1 - side][0])
        def _(side=side):
            move_ends(side).wait_recv()

    def scan_step(j, token):
        for side in range(2):
            @pl.when(sides[1 - side][0])
            def _(side=side):
                move(side, j).wait_recv()

        for side in range(2):
            @pl.when(sides[side][0] & (j == count - 1))
            def _(side=side):
                for i in range(count):
                    move(side, i).wait_send()
                for i in range(count):
                    move_gate(side, i).start()

        scan_slot(
            j, d, source_ref, spans_ref, dtb_ref, alog_ref, skip_ref,
            own_ref, left_ref, right_ref, own_ends, left_ends, right_ends,
            wx_ref, wbc_ref, bx_ref, bbc_ref,
            base_ref, scale_ref, c_ref, end_ref,
            joined, tail, state, decay, mixes, spread, weighted,
        )
        return token

    lax.fori_loop(0, count, scan_step, 0)

    hand = pltpu.make_async_remote_copy(
        end_ref, carried_ref, state_send.at[0], state_recv.at[0],
        device_id={"seq": q + 1}, device_id_type=MESH,
    )

    @pl.when(q < pieces - 1)
    def _():
        hand.start()

    @pl.when(q == 0)
    def _():
        carried_ref[...] = jnp.zeros_like(carried_ref)

    @pl.when(q > 0)
    def _():
        hand.wait_recv()

    beside = ((m > 0, m - 1), (m < groups - 1, m + 1))

    def hop(side, source, j):
        return pltpu.make_async_remote_copy(
            rows.at[source, j], rows.at[source, j],
            (left_send, right_send)[side].at[source, j], arrive.at[source, j],
            device_id={"tensor": m + (2 * side - 1)}, device_id_type=MESH,
        )

    def gate_slot(j):
        for side in range(2):
            @pl.when(sides[1 - side][0])
            def _(side=side):
                move_gate(side, j).wait_recv()

        _, final = slot_row(spans_ref, d, j, count)
        carried = carried_ref[final]
        high = carried.astype(BF16)
        low = (carried - high.astype(F32)).astype(BF16)
        c_act = c_ref[j]
        read = jnp.dot(c_act, high, preferred_element_type=F32) + jnp.dot(
            c_act, low, preferred_element_type=F32
        )
        y = base_ref[j] + scale_ref[j] * read
        parts = [ref[j].astype(F32) for ref in (own_gate, left_gate, right_gate)]
        z = choose(source_ref[d, j], d, *parts)
        g = y * (z / (1.0 + jnp.exp(-z)))
        inverse = lax.rsqrt(jnp.mean(g * g, axis=-1, keepdims=True) + EPS)
        rows[m, j] = (g * inverse * gain_ref[...]).astype(BF16)
        for side, (there, _) in enumerate(beside):
            @pl.when(there)
            def _(side=side):
                hop(side, m, j).start()

    keep.wait()
    for k in range(1, groups):
        arrived(k).wait_recv()

    def project_slot(j):
        for k in range(1, groups):
            for side in range(2):
                source = m - k if side == 1 else m + k
                here = (source >= 0) if side == 1 else (source < groups)

                @pl.when(here)
                def _(side=side, source=source):
                    hop(side, source, j).wait_recv()

                @pl.when(here & beside[side][0])
                def _(side=side, source=source):
                    hop(side, source, j).start()
        total = jnp.dot(rows[0, j], weight_ref[0], preferred_element_type=F32)
        for i in range(1, groups):
            total = total + jnp.dot(rows[i, j], weight_ref[i], preferred_element_type=F32)
        out_ref[j] = total.astype(BF16)

    def turn(j, token):
        @pl.when(j < count)
        def _():
            gate_slot(j)

        @pl.when(j > 0)
        def _():
            project_slot(j - 1)

        return token

    lax.fori_loop(0, count + 1, turn, 0)

    def drain(j, token):
        for side, (there, _) in enumerate(beside):
            @pl.when(there)
            def _(side=side):
                hop(side, m, j).wait_send()
        for k in range(1, groups):
            for side in range(2):
                source = m - k if side == 1 else m + k
                here = (source >= 0) if side == 1 else (source < groups)

                @pl.when(here & beside[side][0])
                def _(side=side, source=source):
                    hop(side, source, j).wait_send()
        return token

    lax.fori_loop(0, count, drain, 0)

    for side in range(2):
        @pl.when(sides[side][0])
        def _(side=side):
            move_ends(side).wait_send()
            for j in range(count):
                move_gate(side, j).wait_send()

    @pl.when(q < pieces - 1)
    def _():
        for copy in tail_copies():
            copy.wait_send()
        hand.wait_send()

    for k in range(1, groups):
        part(k).wait_send()


def body(
    entry_x, entry_z, entry_bc, entry_dt, source_rank, source_slot, row_spans,
    conv_x_weight, conv_x_bias, conv_bc_weight, conv_bc_bias,
    dt_bias, a_log, d_skip, norm_gain, out_weight,
):
    groups = lax.axis_size("tensor")
    count = source_slot.shape[1]
    slots, length, width = entry_x.shape
    bc_width = entry_bc.shape[2]
    full = width + bc_width
    heads, states = width // HEAD, bc_width // 2
    cols = out_weight.shape[1] // groups
    parts = max(groups - 1, 1)
    dma = pltpu.SemaphoreType.DMA
    main = pltpu.VMEM((count, length, full), BF16)
    ends = pltpu.VMEM((count, EXTRA, full), BF16)
    gates = pltpu.VMEM((count, length, width), BF16)
    wide = pltpu.VMEM((count, length, width), F32)
    carry = pltpu.VMEM((count, states, width), F32)
    return pl.pallas_call(
        mixer_kernel,
        in_specs=[SMEM] * 6 + [VMEM] * 9 + [ANY],
        out_specs=VMEM,
        out_shape=jax.ShapeDtypeStruct((count, length, cols), BF16),
        scratch_shapes=[
            main, main, main, ends, ends, ends, pltpu.VMEM((2, count, EXTRA, full), BF16),
            gates, gates, gates,
            pltpu.VMEM((2, count, length, width), BF16),
            pltpu.VMEM((groups, width, cols), BF16),
            pltpu.VMEM((slots, EXTRA, width), BF16),
            pltpu.VMEM((slots, EXTRA, bc_width), BF16),
            pltpu.VMEM((2, count, length, full), BF16),
            wide, wide, pltpu.VMEM((count, length, states), BF16), carry, carry,
            pltpu.VMEM((groups, count, length, width), BF16),
            pltpu.VMEM((length + 8, full), F32),
            pltpu.VMEM((8, full), F32),
            pltpu.VMEM((states, width), F32),
            pltpu.VMEM((1, width), F32),
            pltpu.VMEM((length, heads * length), BF16),
            pltpu.VMEM((heads * length, width), BF16),
            pltpu.VMEM((states, heads * length), BF16),
            dma((2,)), dma((2,)), dma((2, count)), dma((2, count)),
            dma((2, count)), dma((2, count)), dma((parts,)), dma((parts,)), dma((1,)), dma((1,)), dma((1,)),
            dma((groups, count)), dma((groups, count)), dma((groups, count)), dma((2,)), dma((2,)),
        ],
        compiler_params=pltpu.CompilerParams(
            collective_id=0, has_side_effects=True, vmem_limit_bytes=58 << 20
        ),
        name="mixer",
    )(
        source_slot, source_rank, row_spans, dt_bias, a_log, d_skip,
        entry_x, entry_z, entry_bc, jnp.swapaxes(entry_dt, 1, 2),
        conv_x_weight, conv_bc_weight, conv_x_bias.reshape(1, -1), conv_bc_bias.reshape(1, -1),
        norm_gain.reshape(1, -1), out_weight,
    )


def solution(mesh):
    split = P("dp", "seq", "tensor")
    placed = (
        split, split, P("dp", "seq", None), split, P(), P(), P(),
        P(None, "tensor"), P("tensor"), P(), P(),
        P("tensor"), P("tensor"), P("tensor"), P("tensor"), P("tensor", None),
    )
    return jax.shard_map(body, mesh=mesh, in_specs=placed, out_specs=split, check_vma=False)
```
